32 devices in a mesh: parts: 2 (over x), pool: 4 (over y, core), tp: 4 (over z).
Axes of the slice: x: 2, y: 2, z: 4, core: 2. Of those that a mesh axis runs over, the one named last changes fastest.
Arguments:
- residual: bfloat16 [512, 4096], P(('parts', 'pool', 'tp')), parts along dimension 0, may hold values from -6 to 6
- queries: bfloat16 [512, 2048], P(('parts', 'pool'), 'tp'), parts along dimension 0, may hold values from -24 to 24
- new_kv: bfloat16 [2, 512, 1024], P(None, ('parts', 'pool'), 'tp'), parts along dimension 1, may hold values from -4 to 4
- cache: bfloat16 [2, 16, 512, 1024], P(None, ('parts', 'pool'), None, 'tp'), parts along dimension 1, may hold values from -20 to 20
- cache_len: int32 [16], P(('parts', 'pool')), parts along dimension 0, may hold values from 128 to 512, as said below
- draft_count: int32 [16], P(('parts', 'pool')), parts along dimension 0, may hold values from 1 to 32, as said below
- out_proj: bfloat16 [2048, 4096], P('tp'), may hold values from -0.5 to 0.5
- norm_gain: float32 [4096], replicated, may hold values from 0.1 to 1.9
- routes: int32 [512, 2], P(('parts', 'pool', 'tp')), parts along dimension 0, may hold values from 0 to 3, as said below
- slots: int32 [512, 2], P(('parts', 'pool', 'tp')), parts along dimension 0, may hold values from -1 to 11, as said below
- route_weights: bfloat16 [512, 2], P(('parts', 'pool', 'tp')), parts along dimension 0, may hold values from 0.099609375 to 1
- w_gate: bfloat16 [4, 4096, 3200], P('pool', None, 'tp'), may hold values from -0.09375 to 0.09375
- w_up: bfloat16 [4, 4096, 3200], P('pool', None, 'tp'), may hold values from -0.09375 to 0.09375
- w_down: bfloat16 [4, 3200, 4096], P('pool', 'tp'), may hold values from -0.109375 to 0.109375
Outputs:
- mixed: bfloat16 [512, 4096], P(('parts', 'pool', 'tp')), parts along dimension 0
The draws below stay inside these ranges and needn't reach their ends.
There are 2 independent parts, one for each index of `parts`. The reference program is written for one: setup_inputs(seed, part) draws one part's arguments, and reference() takes and returns one part's arrays. A program takes and returns all parts, laid end to end along the dimension named above; an argument that names none is the same for every part. Nothing has to cross between parts.
Inputs may be any that keep to these rules, and one draw needn't show every extreme that they name: `cache_len`: some request has a full cache. `draft_count`: some request has 32 draft rows. `routes`: the 2 ids of a row differ. Within the rows of one device, the routes to one expert taken in order of row and then of k get slots 0, 1, 2 and so on; those past the first 12 get -1; in every draw some expert gets all 12 slots from every device.
All inputs are finite; a program needn't handle non-finite values.
Results may differ from the reference program's by a relative error of at most 0.015.
Values may be sent and summed in bfloat16 or wider, within the bound.
No kernel may reach another device: no remote copies, remote signals or barrier semaphores. Data moves between devices by JAX's collectives and lax.ppermute only.
A program may use at most 64 MiB of HBM per device.

```python
import jax
import jax.numpy as jnp
from jax import lax

D = 4096
HEADS = 16
KV = 8
HD = 128
FF = 3200
TOP = 2
DRAFT = 32
CACHE = 512
EXPERTS = 4
REQS = 8
ROWS = 256
ROW_DEV = 16
CAP = 12
N_TP = 4


def attention_draw(key):
    key_query, key_new, key_cache = jax.random.split(jax.random.fold_in(key, 11), 3)
    query_all = jnp.clip(jax.random.normal(key_query, (REQS, DRAFT, KV, HEADS // KV, HD), jnp.float32), -4.0, 4.0)
    new_all = jnp.clip(jax.random.normal(key_new, (2, REQS * DRAFT, KV * HD), jnp.float32), -4.0, 4.0)
    cache_all = jnp.clip(jax.random.normal(key_cache, (2, REQS, CACHE, KV, HD), jnp.float32), -4.0, 4.0)
    return (query_all.reshape(REQS * DRAFT, HEADS * HD), new_all, cache_all.reshape(2, REQS, CACHE, KV * HD))


def draw_queries(key, part):
    return attention_draw(key)[0].astype(jnp.bfloat16)


def draw_new_kv(key, part):
    return attention_draw(key)[1].astype(jnp.bfloat16)


def draw_cache(key, part):
    return attention_draw(key)[2].astype(jnp.bfloat16)


def draw_cache_len(key, part):
    key_first, key_second = jax.random.split(jax.random.fold_in(key, 23))
    lengths = jax.random.randint(key_first, (REQS,), CACHE // 4, CACHE + 1)
    chosen = jax.random.randint(key_second, (), 0, REQS)
    return jnp.where(jnp.arange(REQS) == chosen, CACHE, lengths).astype(jnp.int32)


def draw_draft_count(key, part):
    key_first, key_second = jax.random.split(jax.random.fold_in(key, 29))
    counts = jax.random.randint(key_first, (REQS,), 1, DRAFT + 1)
    chosen = jax.random.randint(key_second, (), 0, REQS)
    return jnp.where(jnp.arange(REQS) == chosen, DRAFT, counts).astype(jnp.int32)


def route_draw(key):
    key_hot, key_first, key_offset, key_score, key_side = jax.random.split(jax.random.fold_in(key, 31), 5)
    block_count = ROWS // ROW_DEV
    hot_expert = jax.random.randint(key_hot, (), 0, EXPERTS)
    first_pick = jax.random.randint(key_first, (block_count, ROW_DEV), 0, EXPERTS)
    offset = jax.random.randint(key_offset, (block_count, ROW_DEV), 1, EXPERTS)
    second = (first_pick + offset) % EXPERTS
    scores = jax.random.randint(key_score, (block_count, ROW_DEV), 0, 1 << 20) * ROW_DEV + jnp.arange(ROW_DEV)[None, :]
    unused, chosen = lax.top_k(scores, CAP)
    forced = jnp.any(chosen[:, :, None] == jnp.arange(ROW_DEV)[None, None, :], axis=1)
    side_pick = jax.random.randint(key_side, (block_count, ROW_DEV), 0, 2)
    partner = (hot_expert + offset) % EXPERTS
    pick_one = jnp.where(forced, jnp.where(side_pick == 0, hot_expert, partner), first_pick)
    pick_two = jnp.where(forced, jnp.where(side_pick == 0, partner, hot_expert), second)
    route_ids = jnp.stack([pick_one, pick_two], axis=-1).astype(jnp.int32)
    flat_ids = route_ids.reshape(block_count, ROW_DEV * TOP)
    one_hot = (flat_ids[:, :, None] == jnp.arange(EXPERTS)[None, None, :]).astype(jnp.int32)
    running = jnp.cumsum(one_hot, axis=1)
    rank_in = jnp.sum(running * one_hot, axis=-1) - 1
    slot_ids = jnp.where(rank_in < CAP, rank_in, -1)
    return (route_ids.reshape(ROWS, TOP), slot_ids.reshape(ROWS, TOP).astype(jnp.int32))


def draw_routes(key, part):
    return route_draw(key)[0]


def draw_slots(key, part):
    return route_draw(key)[1]


def block_scale(key, dims, pieces, least, high):
    def one(dim, parts):
        steps = jax.random.uniform(jax.random.fold_in(jax.random.fold_in(key, 6), dim), (parts,), jnp.float32, least / len(pieces), high / len(pieces))
        return jnp.repeat(jnp.exp(steps), dims[dim] // parts).reshape((-1,) + (1,) * (len(dims) - dim - 1))

    factor_of = one(*pieces[0])
    for cut in pieces[1:]:
        factor_of = factor_of * one(*cut)
    return factor_of


def bell_draw(stream_key, shape, spread, most, shards=(), dtype=jnp.bfloat16):
    drawn = jax.random.normal(stream_key, shape, jnp.float32) * spread
    if len(shards) > 0:
        drawn = block_scale(stream_key, shape, shards, -0.22, 0.18) * drawn
    return jnp.clip(drawn, min=-most, max=most).astype(dtype)


def setup_inputs(seed: int = 0, part: int = 0) -> dict:
    streams_of = jax.random.split(jax.random.key(seed), 15)
    own_keys = jax.random.split(jax.random.fold_in(streams_of[14], part), 15)
    return {
        "residual": bell_draw(own_keys[0], (ROWS, D), 1.0, 6.0, ((0, 16),)),
        "queries": draw_queries(jax.random.fold_in(jax.random.fold_in(streams_of[14], part), 71), part),
        "new_kv": draw_new_kv(jax.random.fold_in(jax.random.fold_in(streams_of[14], part), 71), part),
        "cache": draw_cache(jax.random.fold_in(jax.random.fold_in(streams_of[14], part), 71), part),
        "cache_len": draw_cache_len(jax.random.fold_in(jax.random.fold_in(streams_of[14], part), 71), part),
        "draft_count": draw_draft_count(jax.random.fold_in(jax.random.fold_in(streams_of[14], part), 71), part),
        "out_proj": bell_draw(streams_of[6], (HEADS * HD, D), HD ** -0.5, 0.5, ((0, 4),)),
        "norm_gain": jnp.clip(1.0 + 0.18 * jax.random.normal(streams_of[7], (D,), jnp.float32), 0.1, 1.9),
        "routes": draw_routes(jax.random.fold_in(jax.random.fold_in(streams_of[14], part), 71), part),
        "slots": draw_slots(jax.random.fold_in(jax.random.fold_in(streams_of[14], part), 71), part),
        "route_weights": jnp.clip(0.099609375 + 0.9003906 * jax.random.uniform(own_keys[10], (ROWS, TOP), jnp.float32) ** block_scale(own_keys[10], (ROWS, TOP), ((0, 16),), -0.2, 0.2), 0.099609375, 1.0).astype(jnp.bfloat16),
        "w_gate": bell_draw(streams_of[11], (EXPERTS, D, FF), D ** -0.5, 0.09375, ((0, 4), (2, 4))),
        "w_up": bell_draw(streams_of[12], (EXPERTS, D, FF), D ** -0.5, 0.09375, ((0, 4), (2, 4))),
        "w_down": bell_draw(streams_of[13], (EXPERTS, FF, D), FF ** -0.5, 0.109375, ((0, 4), (1, 4))),
    }


def reference(residual, queries, new_kv, cache, cache_len, draft_count, out_proj, norm_gain, routes, slots, route_weights, w_gate, w_up, w_down):
    group_size = HEADS // KV
    score_scale = HD ** (-0.5)

    def one_request(bundle):
        query_rows, key_new, value_new, key_old, value_old, length, live_count = bundle
        query_four = query_rows.reshape(DRAFT, KV, group_size, HD).astype(jnp.float32)
        key_new = key_new.reshape(DRAFT, KV, HD).astype(jnp.float32)
        value_new = value_new.reshape(DRAFT, KV, HD).astype(jnp.float32)
        key_old = key_old.reshape(CACHE, KV, HD).astype(jnp.float32)
        value_old = value_old.reshape(CACHE, KV, HD).astype(jnp.float32)
        score_old = jnp.einsum('jkgd,pkd->kgjp', query_four, key_old) * score_scale
        score_new = jnp.einsum('jkgd,ikd->kgji', query_four, key_new) * score_scale
        see_old = jnp.arange(CACHE) < length
        draft_index = jnp.arange(DRAFT)
        see_new = (draft_index[None, :] <= draft_index[:, None]) & (draft_index[None, :] < live_count)
        row_max = jnp.maximum(lax.optimization_barrier(jnp.max(jnp.where(see_old, score_old, -1e+30), axis=-1)), lax.optimization_barrier(jnp.max(jnp.where(see_new, score_new, -1e+30), axis=-1)))
        prob_old = jnp.where(see_old, jnp.exp(score_old - row_max[..., None]), 0.0)
        prob_new = jnp.where(see_new, jnp.exp(score_new - row_max[..., None]), 0.0)
        totals = lax.optimization_barrier(jnp.sum(prob_old, axis=-1)) + lax.optimization_barrier(jnp.sum(prob_new, axis=-1))
        weight_old = lax.optimization_barrier((prob_old / totals[..., None]).astype(jnp.bfloat16)).astype(jnp.float32)
        weight_new = lax.optimization_barrier((prob_new / totals[..., None]).astype(jnp.bfloat16)).astype(jnp.float32)
        output = jnp.einsum('kgjp,pkd->jkgd', weight_old, value_old) + jnp.einsum('kgji,ikd->jkgd', weight_new, value_new)
        return output.reshape(DRAFT, HEADS * HD).astype(jnp.bfloat16)
    attended = lax.map(one_request, (queries.reshape(REQS, DRAFT, HEADS * HD), new_kv[0].reshape(REQS, DRAFT, KV * HD), new_kv[1].reshape(REQS, DRAFT, KV * HD), cache[0], cache[1], cache_len, draft_count)).reshape(ROWS, HEADS * HD)
    projected = jnp.dot(attended, out_proj, preferred_element_type=jnp.float32)
    hidden_state = (residual.astype(jnp.float32) + projected).astype(jnp.bfloat16)
    hidden_wide = hidden_state.astype(jnp.float32)
    power = lax.optimization_barrier(jnp.mean(hidden_wide * hidden_wide, axis=1, keepdims=True))
    normed = (hidden_wide * lax.rsqrt(power + 1e-05) * norm_gain.astype(jnp.float32)).astype(jnp.bfloat16)
    block_count = ROWS // ROW_DEV
    block_of = (jnp.arange(ROWS) // ROW_DEV).astype(jnp.int32)
    is_valid = slots >= 0
    spare = block_count * EXPERTS * CAP
    target = block_of[:, None] * (EXPERTS * CAP) + routes * CAP + slots
    target = jnp.where(is_valid, target, spare).astype(jnp.int32)
    dispatched = jnp.zeros((spare + 1, D), jnp.bfloat16).at[target.reshape(-1)].set(jnp.repeat(normed, TOP, axis=0))
    per_expert = dispatched[:spare].reshape(block_count, EXPERTS, CAP, D).transpose(1, 0, 2, 3).reshape(EXPERTS, block_count * CAP, D)
    slice_width = FF // N_TP

    def serve_rows(bundle):
        row_block, gate_w, up_w, down_w = bundle
        gate_val = jnp.dot(row_block, gate_w, preferred_element_type=jnp.float32)
        up_val = jnp.dot(row_block, up_w, preferred_element_type=jnp.float32)
        activated = (jax.nn.silu(gate_val) * up_val).astype(jnp.bfloat16)
        totals = jnp.zeros((row_block.shape[0], D), jnp.float32)
        for part_index in range(N_TP):
            low_col = part_index * slice_width
            partial_sum = jnp.dot(activated[:, low_col:low_col + slice_width], down_w[low_col:low_col + slice_width], preferred_element_type=jnp.float32)
            totals = totals + lax.optimization_barrier(partial_sum.astype(jnp.bfloat16)).astype(jnp.float32)
        return totals.astype(jnp.bfloat16)
    served = lax.map(serve_rows, (per_expert, w_gate, w_up, w_down))
    flat_out = served.reshape(EXPERTS, block_count, CAP, D).transpose(1, 0, 2, 3).reshape(spare, D)
    flat_out = jnp.concatenate([flat_out, jnp.zeros((1, D), jnp.bfloat16)], axis=0)
    picked = flat_out[target]
    combine_w = jnp.where(is_valid, route_weights.astype(jnp.float32), 0.0)
    moe_sum = lax.optimization_barrier(jnp.sum(picked.astype(jnp.float32) * combine_w[:, :, None], axis=1))
    return (hidden_wide + moe_sum).astype(jnp.bfloat16)
```

```python
import jax
import jax.numpy as jnp
from jax import lax
from jax.sharding import PartitionSpec as P

HD = 128
LANES = 128


def attention(queries, new_kv, cache, cache_len, draft_count):
    requests = cache.shape[1]
    cache_size = cache.shape[2]
    kv_here = cache.shape[3] // HD
    draft_rows = queries.shape[0] // requests
    heads_here = queries.shape[1] // HD
    group_size = heads_here // kv_here
    score_scale = HD ** (-0.5)
    query_blocks = queries.reshape(requests, draft_rows, kv_here, group_size, HD)
    key_old = cache[0].reshape(requests, cache_size, kv_here, HD)
    value_old = cache[1].reshape(requests, cache_size, kv_here, HD)
    key_new = new_kv[0].reshape(requests, draft_rows, kv_here, HD)
    value_new = new_kv[1].reshape(requests, draft_rows, kv_here, HD)
    score_old = (
        jnp.einsum("rjkgd,rpkd->rkgjp", query_blocks, key_old, preferred_element_type=jnp.float32)
        * score_scale
    )
    score_new = (
        jnp.einsum("rjkgd,rikd->rkgji", query_blocks, key_new, preferred_element_type=jnp.float32)
        * score_scale
    )
    see_old = (jnp.arange(cache_size)[None, :] < cache_len[:, None])[:, None, None, None, :]
    draft_index = jnp.arange(draft_rows)
    see_new = (draft_index[None, None, :] <= draft_index[None, :, None]) & (
        draft_index[None, None, :] < draft_count[:, None, None]
    )
    see_new = see_new[:, None, None, :, :]
    row_max = jnp.maximum(
        jnp.max(jnp.where(see_old, score_old, -1e30), axis=-1),
        jnp.max(jnp.where(see_new, score_new, -1e30), axis=-1),
    )
    prob_old = jnp.where(see_old, jnp.exp(score_old - row_max[..., None]), 0.0)
    prob_new = jnp.where(see_new, jnp.exp(score_new - row_max[..., None]), 0.0)
    totals = jnp.sum(prob_old, axis=-1) + jnp.sum(prob_new, axis=-1)
    weight_old = (prob_old / totals[..., None]).astype(jnp.bfloat16)
    weight_new = (prob_new / totals[..., None]).astype(jnp.bfloat16)
    output = jnp.einsum(
        "rkgjp,rpkd->rjkgd", weight_old, value_old, preferred_element_type=jnp.float32
    )
    output = output + jnp.einsum(
        "rkgji,rikd->rjkgd", weight_new, value_new, preferred_element_type=jnp.float32
    )
    return output.reshape(requests * draft_rows, heads_here * HD).astype(jnp.bfloat16)


def wide(x):
    return x.astype(jnp.float32)


def local(
    residual,
    queries,
    new_kv,
    cache,
    cache_len,
    draft_count,
    out_proj,
    norm_gain,
    routes,
    slots,
    route_weights,
    w_gate,
    w_up,
    w_down,
):
    rows, width = residual.shape
    tp = lax.axis_size("tp")
    pool = lax.axis_size("pool")
    cores = 2 if pool % 2 == 0 else 1
    ys = pool // cores
    me_tp = lax.axis_index("tp")
    me_pool = lax.axis_index("pool")

    def from_tp(x, step):
        return lax.ppermute(x, "tp", [((i + step) % tp, i) for i in range(tp)])

    def from_y(x, step):
        return lax.ppermute(
            x, "pool", [((i + step * cores) % pool, i) for i in range(pool)]
        )

    def from_core(x):
        return lax.ppermute(x, "pool", [(i ^ 1, i) for i in range(pool)])

    attended = attention(queries, new_kv, cache, cache_len, draft_count)
    attended = jnp.roll(attended, -me_tp * rows, axis=0)
    partial = jnp.dot(attended, out_proj, preferred_element_type=jnp.float32).astype(jnp.bfloat16)
    total = wide(residual) + wide(partial[:rows])
    for k in range(1, tp):
        total = total + wide(from_tp(partial[k * rows : (k + 1) * rows], tp - k))
    hidden_state = total.astype(jnp.bfloat16)
    hidden_wide = wide(hidden_state)
    power = jnp.mean(hidden_wide * hidden_wide, axis=1, keepdims=True)
    normed = (hidden_wide * lax.rsqrt(power + 1e-05) * norm_gain).astype(jnp.bfloat16)

    lanes = -(-pool // LANES) * LANES
    hit = (routes[:, :, None] == jnp.arange(lanes)) & (slots >= 0)[:, :, None]
    gains = jnp.sum(jnp.where(hit, wide(route_weights)[:, :, None], 0.0), axis=1)
    own = jnp.concatenate([normed, gains.astype(jnp.bfloat16)], axis=1)

    along_tp = [own] + [from_tp(own, k) for k in range(1, tp)]
    along_y = list(along_tp)
    for d in range(1, ys):
        along_y += [from_y(x, d) for x in along_tp]
    half = jnp.concatenate(along_y, axis=0)
    everyone = jnp.concatenate([half, from_core(half)], axis=0) if cores == 2 else half

    gain = wide(jnp.take(everyone[:, width:], me_pool, axis=1))[:, None]
    block = everyone[:, :width]
    gate_val = jnp.dot(block, w_gate[0], preferred_element_type=jnp.float32)
    up_val = jnp.dot(block, w_up[0], preferred_element_type=jnp.float32)
    activated = (jax.nn.silu(gate_val) * up_val * gain).astype(jnp.bfloat16)
    out = jnp.dot(activated, w_down[0], preferred_element_type=jnp.float32).astype(jnp.bfloat16)

    if cores == 2:
        keep = out.shape[0] // 2
        out = (wide(out[:keep]) + wide(from_core(out[keep:]))).astype(jnp.bfloat16)
    keep = tp * rows
    sums = wide(out[:keep])
    for d in range(1, ys):
        sums = sums + wide(from_y(out[d * keep : (d + 1) * keep], ys - d))
    out = sums.astype(jnp.bfloat16)
    mixed = hidden_wide + wide(out[:rows])
    for k in range(1, tp):
        mixed = mixed + wide(from_tp(out[k * rows : (k + 1) * rows], tp - k))
    return mixed.astype(jnp.bfloat16)


def solution(mesh):
    in_specs = (
        P(("parts", "pool", "tp"), None),
        P(("parts", "pool"), "tp"),
        P(None, ("parts", "pool"), "tp"),
        P(None, ("parts", "pool"), None, "tp"),
        P(("parts", "pool")),
        P(("parts", "pool")),
        P("tp", None),
        P(),
        P(("parts", "pool", "tp"), None),
        P(("parts", "pool", "tp"), None),
        P(("parts", "pool", "tp"), None),
        P("pool", None, "tp"),
        P("pool", None, "tp"),
        P("pool", "tp", None),
    )
    out_specs = P(("parts", "pool", "tp"), None)
    return jax.shard_map(local, mesh=mesh, in_specs=in_specs, out_specs=out_specs, check_vma=False)
```

```python
import functools

import jax
import jax.numpy as jnp
from jax import lax
from jax.experimental import pallas as pl
from jax.experimental.pallas import tpu as pltpu
from jax.sharding import PartitionSpec as P

HD = 128
LANES = 128
MIB = 1 << 20
BF = jnp.bfloat16
VMEM = pl.BlockSpec(memory_space=pltpu.VMEM)
SMEM = pl.BlockSpec(memory_space=pltpu.SMEM)
ANY = pl.BlockSpec(memory_space=pl.ANY)


def wide(x):
    return x.astype(jnp.float32)


def dot(a, b):
    return jnp.dot(a, b, preferred_element_type=jnp.float32)


def dot_t(a, b):
    return lax.dot_general(a, b, (((1,), (1,)), ((), ())), preferred_element_type=jnp.float32)


def column_chunks(width, size):
    return [(start, min(size, width - start)) for start in range(0, width, size)]


def attend_body(tp, *refs):
    me, length, count, queries, new_kv, residual, cache, proj = refs[:8]
    outs = refs[8 : 8 + tp]
    cache_in, proj_in, attended, cache_sem, proj_sem = refs[8 + tp :]
    requests, cache_size = cache.shape[1:3]
    draft = queries.shape[0] // requests
    kv_here = cache.shape[3] // HD
    group = queries.shape[1] // HD // kv_here
    rows = residual.shape[0]
    loads = []
    for r in range(requests):
        for side in range(2):
            load = pltpu.make_async_copy(
                cache.at[side, r], cache_in.at[side, r], cache_sem.at[side, r]
            )
            load.start()
            loads.append(load)
    proj_load = pltpu.make_async_copy(proj, proj_in, proj_sem)
    proj_load.start()
    scale = HD ** (-0.5)
    stack = group * draft
    position = lax.broadcasted_iota(jnp.int32, (stack, cache_size), 1)
    key_row = lax.rem(lax.broadcasted_iota(jnp.int32, (stack, draft), 0), draft)
    key_column = lax.broadcasted_iota(jnp.int32, (stack, draft), 1)
    for r in range(requests):
        loads[2 * r].wait()
        loads[2 * r + 1].wait()
        see_old = position < length[r]
        see_new = (key_column <= key_row) & (key_column < count[r])
        draft_rows = slice(r * draft, (r + 1) * draft)
        for k in range(kv_here):
            lanes = slice(k * HD, (k + 1) * HD)
            heads = [k * group + g for g in range(group)]
            query = jnp.concatenate(
                [queries[draft_rows, h * HD : (h + 1) * HD] for h in heads], axis=0
            )
            score_old = dot_t(query, cache_in[0, r, :, lanes]) * scale
            score_new = dot_t(query, new_kv[0, draft_rows, lanes]) * scale
            row_max = jnp.maximum(
                jnp.max(jnp.where(see_old, score_old, -1e30), axis=-1, keepdims=True),
                jnp.max(jnp.where(see_new, score_new, -1e30), axis=-1, keepdims=True),
            )
            prob_old = jnp.where(see_old, jnp.exp(score_old - row_max), 0.0)
            prob_new = jnp.where(see_new, jnp.exp(score_new - row_max), 0.0)
            total = jnp.sum(prob_old, axis=-1, keepdims=True) + jnp.sum(
                prob_new, axis=-1, keepdims=True
            )
            weight_old = (prob_old / total).astype(BF)
            weight_new = (prob_new / total).astype(BF)
            value = dot(weight_old, cache_in[1, r, :, lanes]) + dot(
                weight_new, new_kv[1, draft_rows, lanes]
            )
            for g, h in enumerate(heads):
                attended[draft_rows, h * HD : (h + 1) * HD] = value[g * draft : (g + 1) * draft]
    turned = jnp.concatenate(
        [
            attended[pl.ds(pl.multiple_of(lax.rem(me[0] + k, tp) * rows, rows), rows), :]
            for k in range(tp)
        ],
        axis=0,
    ).astype(BF)
    proj_load.wait()
    for start, size in column_chunks(proj.shape[1], 1024):
        columns = slice(start, start + size)
        part = dot(turned, proj_in[:, columns])
        outs[0][:, columns] = wide(residual[:, columns]) + part[:rows]
        for k in range(1, tp):
            outs[k][:, columns] = part[k * rows : (k + 1) * rows].astype(BF)


def attend(me, length, count, queries, new_kv, residual, cache, proj, tp):
    shape = residual.shape
    return pl.pallas_call(
        functools.partial(attend_body, tp),
        out_shape=[jax.ShapeDtypeStruct(shape, jnp.float32)]
        + [jax.ShapeDtypeStruct(shape, BF)] * (tp - 1),
        in_specs=[SMEM] * 3 + [VMEM] * 3 + [ANY] * 2,
        out_specs=[VMEM] * tp,
        scratch_shapes=[
            pltpu.VMEM(cache.shape, BF),
            pltpu.VMEM(proj.shape, BF),
            pltpu.VMEM(queries.shape, jnp.float32),
            pltpu.SemaphoreType.DMA(cache.shape[:2]),
            pltpu.SemaphoreType.DMA,
        ],
        compiler_params=pltpu.CompilerParams(vmem_limit_bytes=16 * MIB),
        name="attend",
    )(me, length, count, queries, new_kv, residual, cache, proj)


def norm_body(taken, own, *refs):
    others = refs[:taken]
    gain, router, hidden, sent = refs[taken:]
    width = own.shape[1]
    total = own[...]
    for other in others:
        total = total + wide(other[...])
    rounded = total.astype(BF)
    hidden[...] = rounded
    state = wide(rounded)
    power = jnp.mean(state * state, axis=1, keepdims=True)
    sent[:, :width] = (state * lax.rsqrt(power + 1e-05) * gain[...]).astype(BF)
    sent[:, width:] = router[...]


def norm(own, others, gain, router):
    rows, width = own.shape
    return pl.pallas_call(
        functools.partial(norm_body, len(others)),
        out_shape=[
            jax.ShapeDtypeStruct((rows, width), BF),
            jax.ShapeDtypeStruct((rows, width + router.shape[1]), BF),
        ],
        in_specs=[VMEM] * (len(others) + 3),
        out_specs=[VMEM] * 2,
        compiler_params=pltpu.CompilerParams(vmem_limit_bytes=4 * MIB),
        name="norm",
    )(own, *others, gain, router)


def rise_body(taken, me, *refs):
    blocks = refs[:taken]
    gate_w, up_w, activated, held = refs[taken:]
    units, width = gate_w.shape
    start = 0
    gains = []
    for block in blocks:
        size = block.shape[0]
        held[start : start + size, :] = block[:, :width]
        router = block[:, width:]
        mine = lax.broadcasted_iota(jnp.int32, router.shape, 1) == me[1]
        gains.append(jnp.sum(jnp.where(mine, wide(router), 0.0), axis=1, keepdims=True))
        start += size
    gains = gains[0] if taken == 1 else jnp.concatenate(gains, axis=0)
    for top, tall in column_chunks(start, 256):
        rows = held[top : top + tall, :]
        gain = gains[top : top + tall]
        for first, size in column_chunks(units, 256):
            here = slice(first, first + size)
            gate = dot_t(rows, gate_w[here, :])
            up = dot_t(rows, up_w[here, :])
            value = gate / (1.0 + jnp.exp(-gate)) * up * gain
            activated[top : top + tall, here] = value.astype(BF)


def rise(me, blocks, gate_w, up_w):
    units, width = gate_w.shape
    rows = sum(block.shape[0] for block in blocks)
    return pl.pallas_call(
        functools.partial(rise_body, len(blocks)),
        out_shape=jax.ShapeDtypeStruct((rows, units), BF),
        in_specs=[SMEM] + [VMEM] * (len(blocks) + 2),
        out_specs=VMEM,
        scratch_shapes=[pltpu.VMEM((rows, width), BF)],
        compiler_params=pltpu.CompilerParams(vmem_limit_bytes=36 * MIB),
        name="rise",
    )(me, *blocks, gate_w, up_w)


def fall_body(start, activated, down_w, *outs):
    size = outs[0].shape[1]
    for first, wider in column_chunks(size, 512):
        top = 0
        for out in outs:
            tall = out.shape[0]
            value = dot(
                activated[top : top + tall, :], down_w[:, start + first : start + first + wider]
            )
            out[:, first : first + wider] = value.astype(BF)
            top += tall


def fall(activated, down_w, start, size, cores):
    shape = (activated.shape[0] // cores, size)
    return pl.pallas_call(
        functools.partial(fall_body, start),
        out_shape=[jax.ShapeDtypeStruct(shape, BF)] * cores,
        in_specs=[VMEM] * 2,
        out_specs=[VMEM] * cores,
        compiler_params=pltpu.CompilerParams(vmem_limit_bytes=24 * MIB),
        name="fall",
    )(activated, down_w)


def local(
    residual,
    queries,
    new_kv,
    cache,
    cache_len,
    draft_count,
    out_proj,
    norm_gain,
    routes,
    slots,
    route_weights,
    w_gate,
    w_up,
    w_down,
):
    rows, width = residual.shape
    tp = lax.axis_size("tp")
    pool = lax.axis_size("pool")
    cores = 2 if pool % 2 == 0 else 1
    ys = pool // cores
    me = jnp.stack([lax.axis_index("tp"), lax.axis_index("pool")]).astype(jnp.int32)

    def from_tp(x, step):
        return lax.ppermute(x, "tp", [((i + step) % tp, i) for i in range(tp)])

    def from_y(x, step):
        return lax.ppermute(x, "pool", [((i + step * cores) % pool, i) for i in range(pool)])

    def from_core(x):
        return lax.ppermute(x, "pool", [(i ^ 1, i) for i in range(pool)])

    lanes = -(-pool // LANES) * LANES
    hit = (routes[:, :, None] == jnp.arange(lanes)) & (slots >= 0)[:, :, None]
    router = jnp.sum(jnp.where(hit, wide(route_weights)[:, :, None], 0.0), axis=1).astype(BF)

    own, *parts = attend(
        me, cache_len, draft_count, queries, new_kv, residual, cache, out_proj, tp
    )
    taken = [from_tp(part, tp - 1 - k) for k, part in enumerate(parts)]
    hidden_state, sent = norm(own, taken, norm_gain[None, :], router)

    along_tp = [sent] + [from_tp(sent, k) for k in range(1, tp)]
    blocks = list(along_tp)
    for d in range(1, ys):
        blocks += [from_y(x, d) for x in along_tp]
    if cores == 2:
        blocks += [from_core(x) for x in blocks]
    if rows % 16:
        blocks = [jnp.concatenate(blocks, axis=0)]

    gate_w = jnp.swapaxes(w_gate[0], 0, 1)
    up_w = jnp.swapaxes(w_up[0], 0, 1)
    activated = rise(me, blocks, gate_w, up_w)

    mixed = []
    for start, size in column_chunks(width, width // 2):
        out, *other = fall(activated, w_down[0], start, size, cores)
        if other:
            out = (wide(out) + wide(from_core(other[0]))).astype(BF)
        keep = tp * rows
        sums = wide(out[:keep])
        for d in range(1, ys):
            sums = sums + wide(from_y(out[d * keep : (d + 1) * keep], ys - d))
        out = sums.astype(BF)
        total = wide(hidden_state[:, start : start + size]) + wide(out[:rows])
        for k in range(1, tp):
            total = total + wide(from_tp(out[k * rows : (k + 1) * rows], tp - k))
        mixed.append(total.astype(BF))
    return jnp.concatenate(mixed, axis=1)


def solution(mesh):
    in_specs = (
        P(("parts", "pool", "tp"), None),
        P(("parts", "pool"), "tp"),
        P(None, ("parts", "pool"), "tp"),
        P(None, ("parts", "pool"), None, "tp"),
        P(("parts", "pool")),
        P(("parts", "pool")),
        P("tp", None),
        P(),
        P(("parts", "pool", "tp"), None),
        P(("parts", "pool", "tp"), None),
        P(("parts", "pool", "tp"), None),
        P("pool", None, "tp"),
        P("pool", None, "tp"),
        P("pool", "tp", None),
    )
    out_specs = P(("parts", "pool", "tp"), None)
    return jax.shard_map(local, mesh=mesh, in_specs=in_specs, out_specs=out_specs, check_vma=False)
```

```python
import functools

import jax
import jax.numpy as jnp
from jax import lax
from jax.experimental import pallas as pl
from jax.experimental.pallas import tpu as pltpu
from jax.sharding import PartitionSpec as P

HD = 128
LANES = 128
MIB = 1 << 20
BF = jnp.bfloat16
VMEM = pl.BlockSpec(memory_space=pltpu.VMEM)
SMEM = pl.BlockSpec(memory_space=pltpu.SMEM)
ANY = pl.BlockSpec(memory_space=pl.ANY)


def wide(x):
    return x.astype(jnp.float32)


def dot(a, b):
    return jnp.dot(a, b, preferred_element_type=jnp.float32)


def dot_t(a, b):
    return lax.dot_general(a, b, (((1,), (1,)), ((), ())), preferred_element_type=jnp.float32)


def in_hbm(x):
    return pltpu.with_memory_space_constraint(x, pltpu.HBM)


def column_chunks(width, size):
    return [(start, min(size, width - start)) for start in range(0, width, size)]


def attend_body(tp, table, *refs):
    sources = refs[:5]
    outs = refs[5 : 5 + tp]
    queries, new_kv, residual, cache, proj, attended, sems, cache_sems = refs[5 + tp :]
    requests, cache_size = cache.shape[1:3]
    draft = queries.shape[0] // requests
    kv_here = cache.shape[3] // HD
    group = queries.shape[1] // HD // kv_here
    rows = residual.shape[0]
    first = [
        pltpu.make_async_copy(sources[i], target, sems.at[i])
        for i, target in ((0, queries), (1, new_kv))
    ]
    later = [
        pltpu.make_async_copy(sources[i], target, sems.at[i])
        for i, target in ((4, proj), (2, residual))
    ]
    loads = [
        [
            pltpu.make_async_copy(
                sources[3].at[side, r], cache.at[side, r], cache_sems.at[side, r]
            )
            for side in range(2)
        ]
        for r in range(requests)
    ]
    for load in first + sum(loads, []) + later:
        load.start()
    for load in first:
        load.wait()
    scale = HD ** (-0.5)
    stack = group * draft
    position = lax.broadcasted_iota(jnp.int32, (stack, cache_size), 1)
    key_row = lax.rem(lax.broadcasted_iota(jnp.int32, (stack, draft), 0), draft)
    key_column = lax.broadcasted_iota(jnp.int32, (stack, draft), 1)
    for r in range(requests):
        for load in loads[r]:
            load.wait()
        see_old = position < table[2 + r]
        see_new = (key_column <= key_row) & (key_column < table[2 + requests + r])
        draft_rows = slice(r * draft, (r + 1) * draft)
        for k in range(kv_here):
            lanes = slice(k * HD, (k + 1) * HD)
            heads = [k * group + g for g in range(group)]
            query = jnp.concatenate(
                [queries[draft_rows, h * HD : (h + 1) * HD] for h in heads], axis=0
            )
            score_old = dot_t(query, cache[0, r, :, lanes]) * scale
            score_new = dot_t(query, new_kv[0, draft_rows, lanes]) * scale
            row_max = jnp.maximum(
                jnp.max(jnp.where(see_old, score_old, -1e30), axis=-1, keepdims=True),
                jnp.max(jnp.where(see_new, score_new, -1e30), axis=-1, keepdims=True),
            )
            prob_old = jnp.where(see_old, jnp.exp(score_old - row_max), 0.0)
            prob_new = jnp.where(see_new, jnp.exp(score_new - row_max), 0.0)
            total = jnp.sum(prob_old, axis=-1, keepdims=True) + jnp.sum(
                prob_new, axis=-1, keepdims=True
            )
            weight_old = (prob_old / total).astype(BF)
            weight_new = (prob_new / total).astype(BF)
            value = dot(weight_old, cache[1, r, :, lanes]) + dot(
                weight_new, new_kv[1, draft_rows, lanes]
            )
            for g, h in enumerate(heads):
                attended[draft_rows, h * HD : (h + 1) * HD] = value[g * draft : (g + 1) * draft]
    turned = jnp.concatenate(
        [
            attended[pl.ds(pl.multiple_of(lax.rem(table[0] + k, tp) * rows, rows), rows), :]
            for k in range(tp)
        ],
        axis=0,
    ).astype(BF)
    for load in later:
        load.wait()
    for start, size in column_chunks(proj.shape[1], 1024):
        columns = slice(start, start + size)
        part = dot(turned, proj[:, columns])
        outs[0][:, columns] = wide(residual[:, columns]) + part[:rows]
        for k in range(1, tp):
            outs[k][:, columns] = part[k * rows : (k + 1) * rows].astype(BF)


def attend(table, queries, new_kv, residual, cache, proj, tp):
    shape = residual.shape
    sources = (queries, new_kv, residual, cache, proj)
    return pl.pallas_call(
        functools.partial(attend_body, tp),
        out_shape=[jax.ShapeDtypeStruct(shape, jnp.float32)]
        + [jax.ShapeDtypeStruct(shape, BF)] * (tp - 1),
        in_specs=[SMEM] + [ANY] * len(sources),
        out_specs=[VMEM] * tp,
        scratch_shapes=[pltpu.VMEM(x.shape, x.dtype) for x in sources]
        + [
            pltpu.VMEM(queries.shape, jnp.float32),
            pltpu.SemaphoreType.DMA((len(sources),)),
            pltpu.SemaphoreType.DMA(cache.shape[:2]),
        ],
        compiler_params=pltpu.CompilerParams(vmem_limit_bytes=16 * MIB),
        name="attend",
    )(table, *[in_hbm(x) for x in sources])


def hold_body(count, *refs):
    after, sources, outs, done, sems = (
        refs[0], refs[1 : 1 + count], refs[1 + count : 1 + 2 * count], refs[-2], refs[-1]
    )
    del after
    loads = [
        pltpu.make_async_copy(source, out, sems.at[i])
        for i, (source, out) in enumerate(zip(sources, outs))
    ]
    for load in loads:
        load.start()
    done[...] = jnp.zeros_like(done)
    for load in loads:
        load.wait()


def hold(after, arrays):
    size = sum(x.size * x.dtype.itemsize for x in arrays)
    return pl.pallas_call(
        functools.partial(hold_body, len(arrays)),
        out_shape=[pltpu.VMEM(x.shape, x.dtype) for x in arrays]
        + [pltpu.VMEM((8, LANES), jnp.float32)],
        in_specs=[ANY] * (1 + len(arrays)),
        out_specs=[VMEM] * (1 + len(arrays)),
        scratch_shapes=[pltpu.SemaphoreType.DMA((len(arrays),))],
        compiler_params=pltpu.CompilerParams(vmem_limit_bytes=MIB),
        cost_estimate=pl.CostEstimate(flops=0, bytes_accessed=2 * size, transcendentals=0),
        name="hold",
    )(after, *[in_hbm(x) for x in arrays])


def norm_body(taken, token, own, *refs):
    del token
    others = refs[:taken]
    gain, router, hidden, sent = refs[taken:]
    width = own.shape[1]
    total = own[...]
    for other in others:
        total = total + wide(other[...])
    rounded = total.astype(BF)
    hidden[...] = rounded
    state = wide(rounded)
    power = jnp.mean(state * state, axis=1, keepdims=True)
    sent[:, :width] = (state * lax.rsqrt(power + 1e-05) * gain[...]).astype(BF)
    sent[:, width:] = router[...]


def norm(token, own, others, gain, router):
    rows, width = own.shape
    return pl.pallas_call(
        functools.partial(norm_body, len(others)),
        out_shape=[
            jax.ShapeDtypeStruct((rows, width), BF),
            jax.ShapeDtypeStruct((rows, width + router.shape[1]), BF),
        ],
        in_specs=[ANY] + [VMEM] * (len(others) + 3),
        out_specs=[VMEM] * 2,
        compiler_params=pltpu.CompilerParams(vmem_limit_bytes=4 * MIB),
        name="norm",
    )(token, own, *others, gain, router)


def rise_body(taken, me, *refs):
    blocks = refs[:taken]
    gate_w, up_w, activated, held = refs[taken:]
    units, width = gate_w.shape
    start = 0
    gains = []
    for block in blocks:
        size = block.shape[0]
        held[start : start + size, :] = block[:, :width]
        router = block[:, width:]
        mine = lax.broadcasted_iota(jnp.int32, router.shape, 1) == me[1]
        gains.append(jnp.sum(jnp.where(mine, wide(router), 0.0), axis=1, keepdims=True))
        start += size
    gains = gains[0] if taken == 1 else jnp.concatenate(gains, axis=0)
    for top, tall in column_chunks(start, 256):
        rows = held[top : top + tall, :]
        gain = gains[top : top + tall]
        for first, size in column_chunks(units, 256):
            here = slice(first, first + size)
            gate = dot_t(rows, gate_w[here, :])
            up = dot_t(rows, up_w[here, :])
            value = gate / (1.0 + jnp.exp(-gate)) * up * gain
            activated[top : top + tall, here] = value.astype(BF)


def rise(me, blocks, gate_w, up_w):
    units, width = gate_w.shape
    rows = sum(block.shape[0] for block in blocks)
    return pl.pallas_call(
        functools.partial(rise_body, len(blocks)),
        out_shape=jax.ShapeDtypeStruct((rows, units), BF),
        in_specs=[SMEM] + [VMEM] * (len(blocks) + 2),
        out_specs=VMEM,
        scratch_shapes=[pltpu.VMEM((rows, width), BF)],
        compiler_params=pltpu.CompilerParams(vmem_limit_bytes=8 * MIB),
        name="rise",
    )(me, *blocks, gate_w, up_w)


def fall_body(start, activated, down_w, *outs):
    size = outs[0].shape[1]
    for first, wider in column_chunks(size, 512):
        top = 0
        for out in outs:
            tall = out.shape[0]
            value = dot(
                activated[top : top + tall, :], down_w[:, start + first : start + first + wider]
            )
            out[:, first : first + wider] = value.astype(BF)
            top += tall


def fall(activated, down_w, start, size, cores):
    shape = (activated.shape[0] // cores, size)
    return pl.pallas_call(
        functools.partial(fall_body, start),
        out_shape=[jax.ShapeDtypeStruct(shape, BF)] * cores,
        in_specs=[VMEM] * 2,
        out_specs=[VMEM] * cores,
        compiler_params=pltpu.CompilerParams(vmem_limit_bytes=4 * MIB),
        name="fall",
    )(activated, down_w)


def local(
    residual,
    queries,
    new_kv,
    cache,
    cache_len,
    draft_count,
    out_proj,
    norm_gain,
    routes,
    slots,
    route_weights,
    w_gate,
    w_up,
    w_down,
):
    rows, width = residual.shape
    tp = lax.axis_size("tp")
    pool = lax.axis_size("pool")
    cores = 2 if pool % 2 == 0 else 1
    ys = pool // cores
    me = jnp.stack([lax.axis_index("tp"), lax.axis_index("pool")]).astype(jnp.int32)
    table = jnp.concatenate([me, cache_len, draft_count])

    def from_tp(x, step):
        return lax.ppermute(x, "tp", [((i + step) % tp, i) for i in range(tp)])

    def from_y(x, step):
        return lax.ppermute(x, "pool", [((i + step * cores) % pool, i) for i in range(pool)])

    def from_core(x):
        return lax.ppermute(x, "pool", [(i ^ 1, i) for i in range(pool)])

    lanes = -(-pool // LANES) * LANES
    hit = (routes[:, :, None] == jnp.arange(lanes)) & (slots >= 0)[:, :, None]
    router = jnp.sum(jnp.where(hit, wide(route_weights)[:, :, None], 0.0), axis=1).astype(BF)

    own, *parts = attend(table, queries, new_kv, residual, cache, out_proj, tp)
    taken = [from_tp(part, tp - 1 - k) for k, part in enumerate(parts)]
    gate_w = jnp.swapaxes(w_gate[0], 0, 1)
    up_w = jnp.swapaxes(w_up[0], 0, 1)
    gate_w, up_w, down_w, token = hold(own, [gate_w, up_w, w_down[0]])
    hidden_state, sent = norm(token, own, taken, norm_gain[None, :], router)

    along_tp = [sent] + [from_tp(sent, k) for k in range(1, tp)]
    blocks = list(along_tp)
    for d in range(1, ys):
        blocks += [from_y(x, d) for x in along_tp]
    if cores == 2:
        blocks += [from_core(x) for x in blocks]
    if rows % 16:
        blocks = [jnp.concatenate(blocks, axis=0)]

    activated = rise(table, blocks, gate_w, up_w)

    mixed = []
    for start, size in column_chunks(width, width // 2):
        out, *other = fall(activated, down_w, start, size, cores)
        if other:
            out = (wide(out) + wide(from_core(other[0]))).astype(BF)
        keep = tp * rows
        sums = wide(out[:keep])
        for d in range(1, ys):
            sums = sums + wide(from_y(out[d * keep : (d + 1) * keep], ys - d))
        out = sums.astype(BF)
        total = wide(hidden_state[:, start : start + size]) + wide(out[:rows])
        for k in range(1, tp):
            total = total + wide(from_tp(out[k * rows : (k + 1) * rows], tp - k))
        mixed.append(total.astype(BF))
    return jnp.concatenate(mixed, axis=1)


def solution(mesh):
    in_specs = (
        P(("parts", "pool", "tp"), None),
        P(("parts", "pool"), "tp"),
        P(None, ("parts", "pool"), "tp"),
        P(None, ("parts", "pool"), None, "tp"),
        P(("parts", "pool")),
        P(("parts", "pool")),
        P("tp", None),
        P(),
        P(("parts", "pool", "tp"), None),
        P(("parts", "pool", "tp"), None),
        P(("parts", "pool", "tp"), None),
        P("pool", None, "tp"),
        P("pool", None, "tp"),
        P("pool", "tp", None),
    )
    out_specs = P(("parts", "pool", "tp"), None)
    return jax.shard_map(local, mesh=mesh, in_specs=in_specs, out_specs=out_specs, check_vma=False)
```
